32 devices in a mesh: tok: 4 (over x, core), inc: 2 (over y), outc: 4 (over z).
Axes of the slice: x: 2, y: 2, z: 4, core: 2. Of those that a mesh axis runs over, the one named last changes fastest.
Arguments:
- activations: bfloat16 [2, 1024, 8192], P(None, 'tok', 'inc'), may hold values from -0.119628906 to 0.119628906
- student_out: bfloat16 [2, 1024, 4096], P(None, ('tok', 'inc'), 'outc'), may hold values from -6 to 6
- teacher_out: bfloat16 [2, 1024, 4096], P(None, ('tok', 'inc'), 'outc'), may hold values from -6 to 6
- weight: bfloat16 [2, 4096, 4096], P('inc', 'tok', 'outc'), may hold values from -0.0625 to 0.0625
Outputs:
- input_grad: bfloat16 [2, 1024, 8192], P(None, ('tok', 'outc'), 'inc')
- weight_grad: float32 [2, 4096, 4096], P('inc', 'tok', 'outc')
The draws below stay inside these ranges and needn't reach their ends.
All inputs are finite; a program needn't handle non-finite values.
Results may differ from the reference program's by a relative error of at most 0.0051.
Values may be sent and summed in bfloat16 or wider, within the bound.
A program may use at most 128 MiB of HBM per device.

```python
import jax
import jax.numpy as jnp

DIN = 8192
DOUT = 4096
MB = 2
TOKENS = 1024
INGROUPS = 2
IN_BLK = 4096


def with_spikes(entries, key, source, target, shards_of, factor):
    owner, partner = [(jnp.arange(entries.shape[dim]) // (entries.shape[dim] // shards_of)).reshape([-1 if axis == dim else 1 for axis in range(entries.ndim)]) for dim in (source, target)]
    chosen = jax.random.permutation(key, shards_of)[partner]
    strong = (owner == chosen) | (owner == (partner + shards_of // 2) % shards_of)
    return jnp.where(strong, factor * entries, entries)


def block_levels(own_key, dims, split, low, top_value):
    gain, own = 1.0, jax.random.fold_in(own_key, 6)
    for axis_at, shards_of in split:
        steps = jnp.exp(jax.random.uniform(jax.random.fold_in(own, axis_at), (shards_of,), jnp.float32, low / len(split), top_value / len(split)))
        gain = gain * jnp.repeat(steps, dims[axis_at] // shards_of).reshape([-1 if axis == axis_at else 1 for axis in range(len(dims))])
    return gain


def gaussian(stream_key, dims, width, bound, pieces=(), dtype=jnp.bfloat16):
    result = jax.random.normal(stream_key, dims, jnp.float32) * width
    if len(pieces) > 0:
        result = block_levels(stream_key, dims, pieces, -0.22, 0.18) * result
    return jnp.clip(result, min=-bound, max=bound).astype(dtype)


def bell_draw_with(rng, dims, spread, reach, shards, heavy, held_as=jnp.bfloat16):
    drawn = spread * jax.random.normal(rng, dims, jnp.float32)
    if shards:
        drawn = drawn * block_levels(rng, dims, shards, -0.22, 0.18)
    return jnp.clip(with_spikes(drawn, jax.random.fold_in(rng, 3), *heavy), -reach, reach).astype(held_as)


def setup_inputs(seed: int = 0) -> dict:
    seeds = jax.random.split(jax.random.key(seed), 5)
    activations = bell_draw_with(seeds[0], (MB, TOKENS, DIN), 0.02, 0.119628906, ((1, 4), (2, 2)), (1, 2, 4, 2.0))
    student_out = gaussian(seeds[1], (MB, TOKENS, DOUT), 1.0, 6.0, ((1, 8), (2, 4)))
    teacher_out = gaussian(seeds[2], (MB, TOKENS, DOUT), 1.0, 6.0, ((1, 8), (2, 4)))
    weight = gaussian(seeds[3], (INGROUPS, IN_BLK, DOUT), DIN ** -0.5, 0.0625, ((0, 2), (1, 4), (2, 4)))
    return {"activations": activations, "student_out": student_out, "teacher_out": teacher_out, "weight": weight}


def reference(activations, student_out, teacher_out, weight):
    difference = (student_out.astype(jnp.float32) - teacher_out.astype(jnp.float32)).astype(jnp.bfloat16)
    full_weight = weight.reshape(INGROUPS * IN_BLK, DOUT)
    input_grad = jnp.einsum("mtc,rc->mtr", difference.astype(jnp.float32), full_weight.astype(jnp.float32)).astype(jnp.bfloat16)
    weight_grad = jnp.einsum("mti,mtc->ic", activations.astype(jnp.float32), difference.astype(jnp.float32))
    return input_grad, weight_grad.reshape(INGROUPS, IN_BLK, DOUT)
```

```python
import functools

import jax
import jax.numpy as jnp
from jax import lax
from jax.experimental import pallas as pl
from jax.experimental.pallas import tpu as pltpu
from jax.sharding import PartitionSpec as P

MESH = pl.DeviceIdType.MESH


def kernel(
    sizes,
    act,
    student,
    teacher,
    weight,
    dx_out,
    dw_out,
    cot,
    acts,
    part,
    recv,
    sendbuf,
    landing,
    dw,
    w,
    cot_core_s,
    cot_tok_s,
    cot_inc_s,
    cot_r,
    act_s,
    act_r,
    line_s,
    line_r,
    fin_s,
    fin_r,
    out_s,
    misc_s,
):
    n_tok, n_inc, n_out = sizes
    pairs = n_tok // 2
    per_block = n_out // n_inc
    blocks = n_tok * n_inc
    feats = dw.shape[0]
    i, j, k = lax.axis_index("tok"), lax.axis_index("inc"), lax.axis_index("outc")
    p, c = i // 2, i % 2
    f_tile = min(256, feats)

    def tok_at(dp, dc):
        return lax.rem(p + dp, pairs) * 2 + lax.rem(c + dc, 2)

    def inc_at(dj):
        return lax.rem(j + dj, n_inc)

    barrier = pltpu.get_barrier_semaphore()
    for d in range(1, n_tok):
        pl.semaphore_signal(
            barrier, inc=1, device_id={"tok": lax.rem(i + d, n_tok)}, device_id_type=MESH
        )
    for d in range(1, n_inc):
        pl.semaphore_signal(barrier, inc=1, device_id={"inc": inc_at(d)}, device_id_type=MESH)

    @pl.when(k > 0)
    def _():
        pl.semaphore_signal(barrier, inc=1, device_id={"outc": k - 1}, device_id_type=MESH)

    @pl.when(k < n_out - 1)
    def _():
        pl.semaphore_signal(barrier, inc=1, device_id={"outc": k + 1}, device_id_type=MESH)

    own = i * n_inc + j
    w_copy = pltpu.make_async_copy(weight, w, misc_s.at[0])
    w_copy.start()
    act_copy = pltpu.make_async_copy(
        act.at[:, :, pl.ds(pl.multiple_of(i * feats, feats), feats)], acts.at[i], misc_s.at[1]
    )
    act_copy.start()
    cot[own] = (student[...].astype(jnp.float32) - teacher[...].astype(jnp.float32)).astype(
        jnp.bfloat16
    )

    @pl.loop(0, feats // f_tile)
    def _(t):
        rows = pl.ds(pl.multiple_of(t * f_tile, f_tile), f_tile)
        dw[rows, :] = jnp.zeros((f_tile, dw.shape[1]), jnp.float32)

    edges = jnp.where(k > 0, 1, 0) + jnp.where(k < n_out - 1, 1, 0)
    pl.semaphore_wait(barrier, n_tok - 1 + n_inc - 1 + edges)

    def cot_copy(g, sem, device):
        return pltpu.make_async_remote_copy(
            src_ref=cot.at[g],
            dst_ref=cot.at[g],
            send_sem=sem,
            recv_sem=cot_r.at[g],
            device_id=device,
            device_id_type=MESH,
        )

    core = {"tok": tok_at(0, 1)}

    def to_core(g):
        return cot_copy(g, cot_core_s.at[g], core)

    def to_tok(dp):
        return cot_copy(own, cot_tok_s.at[dp], {"tok": tok_at(dp, 0)})

    def to_inc(dp, dj):
        g = tok_at(dp, 0) * n_inc + j
        return cot_copy(g, cot_inc_s.at[dp * n_inc + dj], {"inc": inc_at(dj)})

    def act_send(dp, dc):
        to = tok_at(dp, dc)
        return pltpu.make_async_remote_copy(
            src_ref=act.at[:, :, pl.ds(pl.multiple_of(to * feats, feats), feats)],
            dst_ref=acts.at[i],
            send_sem=act_s.at[dp * 2 + dc],
            recv_sem=act_r.at[i],
            device_id={"tok": to},
            device_id_type=MESH,
        )

    to_core(own).start()
    for dp in range(1, pairs):
        to_tok(dp).start()
    for dj in range(1, n_inc):
        to_inc(0, dj).start()
    for dp in range(pairs):
        for dc in range(2):
            if dp or dc:
                act_send(dp, dc).start()
    w_copy.wait()

    def block_of(b):
        dc, rest = b % 2, b // 2
        dj, dp = rest % n_inc, rest // n_inc
        to, jj = tok_at(dp, dc), inc_at(dj)
        return to, jj, to * n_inc + jj, dc

    def line_copy(item, down):
        return pltpu.make_async_remote_copy(
            src_ref=sendbuf.at[item],
            dst_ref=recv.at[down, item],
            send_sem=line_s.at[item],
            recv_sem=line_r.at[down, item],
            device_id={"outc": k + 1 - 2 * down},
            device_id_type=MESH,
        )

    def line_wait(item, down):
        pltpu.make_async_remote_copy(
            src_ref=sendbuf.at[item],
            dst_ref=recv.at[down, item],
            send_sem=line_s.at[item],
            recv_sem=line_r.at[down, item],
            device_id={"outc": lax.rem(k + 1, n_out)},
            device_id_type=MESH,
        ).wait_recv()

    at_edge = (k == 0) | (k == n_out - 1)

    def compute(b):
        to, jj, g, dc = block_of(b)

        @pl.when(dc == 1)
        def _():
            to_core(g).wait_recv()

        rows = cot[g]
        n_mb, n_rows, depth = rows.shape
        rows = rows.reshape(n_mb * n_rows, depth)

        @pl.loop(0, feats // f_tile)
        def _(t):
            cols = pl.ds(pl.multiple_of(t * f_tile, f_tile), f_tile)
            res = lax.dot_general(
                cot[g].reshape(n_mb * n_rows, depth),
                w[0, cols, :],
                (((1,), (1,)), ((), ())),
                preferred_element_type=jnp.float32,
            ).reshape(n_mb, per_block, n_rows // per_block, f_tile)
            for s in range(per_block):
                part[g * per_block + s, :, :, cols] = res[:, s]

        @pl.when(at_edge)
        def _():
            @pl.loop(0, per_block)
            def _(s):
                item = g * per_block + s
                target = jj * per_block + s

                @pl.when(target != k)
                def _():
                    sendbuf[item] = part[item].astype(jnp.bfloat16)
                    line_copy(item, jnp.where(target < k, 1, 0)).start()

    def fin_copy(to):
        return pltpu.make_async_remote_copy(
            src_ref=sendbuf.at[to * n_out + k],
            dst_ref=landing.at[i],
            send_sem=fin_s.at[to],
            recv_sem=fin_r.at[i],
            device_id={"tok": to},
            device_id_type=MESH,
        )

    def relay(b):
        to, jj, g, dc = block_of(b)

        @pl.loop(0, per_block)
        def _(s):
            item = g * per_block + s
            target = jj * per_block + s

            @pl.when((target != k) & jnp.logical_not(at_edge))
            def _():
                down = jnp.where(target < k, 1, 0)
                line_wait(item, down)
                sendbuf[item] = (part[item] + recv[down, item].astype(jnp.float32)).astype(
                    jnp.bfloat16
                )
                line_copy(item, down).start()

            @pl.when(target == k)
            def _():
                @pl.when(k > 0)
                def _():
                    line_wait(item, 0)
                    part[item] = part[item] + recv[0, item].astype(jnp.float32)

                @pl.when(k < n_out - 1)
                def _():
                    line_wait(item, 1)
                    part[item] = part[item] + recv[1, item].astype(jnp.float32)

                @pl.when(to == i)
                def _():
                    landing[i] = part[item].astype(jnp.bfloat16)

                @pl.when(to != i)
                def _():
                    sendbuf[item] = part[item].astype(jnp.bfloat16)
                    fin_copy(to).start()

    def weight_term(dp, dc):
        to = tok_at(dp, dc)
        if dp or dc:
            pltpu.make_async_remote_copy(
                src_ref=acts.at[to],
                dst_ref=acts.at[to],
                send_sem=act_s.at[dp * 2 + dc],
                recv_sem=act_r.at[to],
                device_id={"tok": tok_at(0, 1)},
                device_id_type=MESH,
            ).wait_recv()
        else:
            act_copy.wait()

    def weight_dot(to):
        @pl.loop(0, feats // f_tile)
        def _(t):
            cols = pl.ds(pl.multiple_of(t * f_tile, f_tile), f_tile)
            n_mb = acts.shape[1]
            lhs = acts[to, :, :, cols].reshape(-1, f_tile)
            rhs = jnp.concatenate(
                [cot[to * n_inc + jj, m] for m in range(n_mb) for jj in range(n_inc)], axis=0
            )
            dw[cols, :] += lax.dot_general(
                lhs, rhs, (((0,), (0,)), ((), ())), preferred_element_type=jnp.float32
            )

    def run(fn, low, high):
        @pl.loop(low, high)
        def _(b):
            fn(b)

    first = 2 * n_inc + 2
    run(compute, 0, 2)
    for dp in range(1, pairs):
        g = tok_at(dp, 0) * n_inc + j
        to_core(g).wait_recv()
        for dj in range(1, n_inc):
            to_inc(dp, dj).start()
        to_core(g).start()
    for dj in range(1, n_inc):
        g = i * n_inc + inc_at(dj)
        to_core(g).wait_recv()
        to_core(g).start()
    run(compute, 2, first)
    run(relay, 0, 2)
    for dp in range(1, pairs):
        for dj in range(1, n_inc):
            g = tok_at(dp, 0) * n_inc + inc_at(dj)
            to_core(g).wait_recv()
            to_core(g).start()
    run(compute, first, blocks)
    for dc in range(2):
        weight_term(0, dc)
        weight_dot(tok_at(0, dc))
    run(relay, 2, first)
    for dp in range(1, pairs):
        for dc in range(2):
            weight_term(dp, dc)
    run(lambda d: weight_dot(tok_at(d // 2, d % 2)), 2, n_tok)
    dw_copy = pltpu.make_async_copy(dw, dw_out.at[0], misc_s.at[2])
    dw_copy.start()
    run(relay, first, blocks)

    def out_copy(frm):
        return pltpu.make_async_copy(
            landing.at[frm],
            dx_out.at[:, :, pl.ds(pl.multiple_of(frm * feats, feats), feats)],
            out_s.at[frm],
        )

    out_copy(i).start()
    for d in range(1, n_tok):
        frm = lax.rem(i + d, n_tok)
        pltpu.make_async_remote_copy(
            src_ref=landing.at[frm],
            dst_ref=landing.at[frm],
            send_sem=fin_s.at[frm],
            recv_sem=fin_r.at[frm],
            device_id={"tok": frm},
            device_id_type=MESH,
        ).wait_recv()
        out_copy(frm).start()

    for dp in range(pairs):
        for dj in range(n_inc):
            to_core(tok_at(dp, 0) * n_inc + inc_at(dj)).wait_send()
            if dj:
                to_inc(dp, dj).wait_send()
        if dp:
            to_tok(dp).wait_send()
        for dc in range(2):
            if dp or dc:
                act_send(dp, dc).wait_send()

    @pl.loop(0, n_tok * n_out)
    def _(item):
        @pl.when(item % n_out != k)
        def _():
            down = jnp.where(item % n_out < k, 1, 0)
            line_copy(item, down).wait_send()

    for d in range(1, n_tok):
        fin_copy(lax.rem(i + d, n_tok)).wait_send()
    for d in range(n_tok):
        out_copy(lax.rem(i + d, n_tok)).wait()
    dw_copy.wait()


def solution(mesh):
    sizes = tuple(mesh.shape[name] for name in ("tok", "inc", "outc"))
    n_tok, n_inc, n_out = sizes

    def local(activations, student_out, teacher_out, weight):
        n_mb, rows, depth = student_out.shape
        feats = weight.shape[1]
        chunk = rows * n_inc // n_out
        items = n_tok * n_out
        bf16, f32 = jnp.bfloat16, jnp.float32
        dma = pltpu.SemaphoreType.DMA
        flops = 4 * n_mb * rows * n_inc * n_tok * depth * feats
        return pl.pallas_call(
            functools.partial(kernel, sizes),
            out_shape=(
                jax.ShapeDtypeStruct((n_mb, chunk, n_tok * feats), bf16),
                jax.ShapeDtypeStruct(weight.shape, f32),
            ),
            in_specs=[
                pl.BlockSpec(memory_space=pl.ANY),
                pl.BlockSpec(memory_space=pltpu.VMEM),
                pl.BlockSpec(memory_space=pltpu.VMEM),
                pl.BlockSpec(memory_space=pl.ANY),
            ],
            out_specs=(pl.BlockSpec(memory_space=pl.ANY), pl.BlockSpec(memory_space=pl.ANY)),
            scratch_shapes=[
                pltpu.VMEM((n_tok * n_inc, n_mb, rows, depth), bf16),
                pltpu.VMEM((n_tok, n_mb, activations.shape[1], feats), bf16),
                pltpu.VMEM((items, n_mb, chunk, feats), f32),
                pltpu.VMEM((2, items, n_mb, chunk, feats), bf16),
                pltpu.VMEM((items, n_mb, chunk, feats), bf16),
                pltpu.VMEM((n_tok, n_mb, chunk, feats), bf16),
                pltpu.VMEM((feats, depth), f32),
                pltpu.VMEM(weight.shape, bf16),
                dma((n_tok * n_inc,)),
                dma((n_tok // 2,)),
                dma((n_tok // 2 * n_inc,)),
                dma((n_tok * n_inc,)),
                dma((n_tok,)),
                dma((n_tok,)),
                dma((items,)),
                dma((2, items)),
                dma((n_tok,)),
                dma((n_tok,)),
                dma((n_tok,)),
                dma((3,)),
            ],
            compiler_params=pltpu.CompilerParams(
                collective_id=0, has_side_effects=True, vmem_limit_bytes=62 * 1024 * 1024
            ),
            cost_estimate=pl.CostEstimate(
                flops=flops, bytes_accessed=16 * 1024 * 1024, transcendentals=0
            ),
        )(activations, student_out, teacher_out, weight)

    placed = (
        P(None, "tok", "inc"),
        P(None, ("tok", "inc"), "outc"),
        P(None, ("tok", "inc"), "outc"),
        P("inc", "tok", "outc"),
    )
    return jax.shard_map(
        local,
        mesh=mesh,
        in_specs=placed,
        out_specs=(P(None, ("tok", "outc"), "inc"), P("inc", "tok", "outc")),
        check_vma=False,
    )
```

```python
import functools

import jax
import jax.numpy as jnp
from jax import lax
from jax.experimental import pallas as pl
from jax.experimental.pallas import tpu as pltpu
from jax.sharding import PartitionSpec as P

MESH = pl.DeviceIdType.MESH


def kernel(
    sizes,
    act,
    student,
    teacher,
    weight,
    dx_out,
    dw_out,
    cot,
    acts,
    part,
    recv,
    sendbuf,
    landing,
    dw,
    w,
    cot_core_s,
    cot_tok_s,
    cot_inc_s,
    cot_r,
    act_s,
    act_r,
    line_s,
    line_r,
    fin_s,
    fin_r,
    out_s,
    misc_s,
):
    n_tok, n_inc, n_out = sizes
    pairs = n_tok // 2
    per_block = n_out // n_inc
    blocks = n_tok * n_inc
    feats = dw.shape[0]
    i, j, k = lax.axis_index("tok"), lax.axis_index("inc"), lax.axis_index("outc")
    p, c = i // 2, i % 2
    f_tile = min(256, feats)

    def tok_at(dp, dc):
        return lax.rem(p + dp, pairs) * 2 + lax.rem(c + dc, 2)

    def inc_at(dj):
        return lax.rem(j + dj, n_inc)

    barrier = pltpu.get_barrier_semaphore()
    for d in range(1, n_tok):
        pl.semaphore_signal(
            barrier, inc=1, device_id={"tok": lax.rem(i + d, n_tok)}, device_id_type=MESH
        )
    for d in range(1, n_inc):
        pl.semaphore_signal(barrier, inc=1, device_id={"inc": inc_at(d)}, device_id_type=MESH)

    @pl.when(k > 0)
    def _():
        pl.semaphore_signal(barrier, inc=1, device_id={"outc": k - 1}, device_id_type=MESH)

    @pl.when(k < n_out - 1)
    def _():
        pl.semaphore_signal(barrier, inc=1, device_id={"outc": k + 1}, device_id_type=MESH)

    own = i * n_inc + j
    w_copy = pltpu.make_async_copy(weight, w, misc_s.at[0])
    w_copy.start()
    act_copy = pltpu.make_async_copy(
        act.at[:, :, pl.ds(pl.multiple_of(i * feats, feats), feats)], acts.at[i], misc_s.at[1]
    )
    act_copy.start()
    cot[own] = (student[...].astype(jnp.float32) - teacher[...].astype(jnp.float32)).astype(
        jnp.bfloat16
    )

    @pl.loop(0, feats // f_tile)
    def _(t):
        rows = pl.ds(pl.multiple_of(t * f_tile, f_tile), f_tile)
        dw[rows, :] = jnp.zeros((f_tile, dw.shape[1]), jnp.float32)

    edges = jnp.where(k > 0, 1, 0) + jnp.where(k < n_out - 1, 1, 0)
    pl.semaphore_wait(barrier, n_tok - 1 + n_inc - 1 + edges)

    def cot_copy(g, sem, device):
        return pltpu.make_async_remote_copy(
            src_ref=cot.at[g],
            dst_ref=cot.at[g],
            send_sem=sem,
            recv_sem=cot_r.at[g],
            device_id=device,
            device_id_type=MESH,
        )

    core = {"tok": tok_at(0, 1)}

    def to_core(g):
        return cot_copy(g, cot_core_s.at[g], core)

    def to_tok(dp):
        return cot_copy(own, cot_tok_s.at[dp], {"tok": tok_at(dp, 0)})

    def to_inc(dp, dj):
        g = tok_at(dp, 0) * n_inc + j
        return cot_copy(g, cot_inc_s.at[dp * n_inc + dj], {"inc": inc_at(dj)})

    def act_send(dp, dc):
        to = tok_at(dp, dc)
        return pltpu.make_async_remote_copy(
            src_ref=act.at[:, :, pl.ds(pl.multiple_of(to * feats, feats), feats)],
            dst_ref=acts.at[i],
            send_sem=act_s.at[dp * 2 + dc],
            recv_sem=act_r.at[i],
            device_id={"tok": to},
            device_id_type=MESH,
        )

    to_core(own).start()
    for dp in range(1, pairs):
        to_tok(dp).start()
    for dj in range(1, n_inc):
        to_inc(0, dj).start()
    for dp in range(pairs):
        for dc in range(2):
            if dp or dc:
                act_send(dp, dc).start()
    w_copy.wait()

    def block_of(b):
        dc, rest = b % 2, b // 2
        dj, dp = rest % n_inc, rest // n_inc
        to, jj = tok_at(dp, dc), inc_at(dj)
        return to, jj, to * n_inc + jj, dc

    def line_copy(item, down):
        return pltpu.make_async_remote_copy(
            src_ref=sendbuf.at[item],
            dst_ref=recv.at[down, item],
            send_sem=line_s.at[item],
            recv_sem=line_r.at[down, item],
            device_id={"outc": k + 1 - 2 * down},
            device_id_type=MESH,
        )

    def line_wait(item, down):
        pltpu.make_async_remote_copy(
            src_ref=sendbuf.at[item],
            dst_ref=recv.at[down, item],
            send_sem=line_s.at[item],
            recv_sem=line_r.at[down, item],
            device_id={"outc": lax.rem(k + 1, n_out)},
            device_id_type=MESH,
        ).wait_recv()

    at_edge = (k == 0) | (k == n_out - 1)

    def compute(b):
        to, jj, g, dc = block_of(b)

        @pl.when(dc == 1)
        def _():
            to_core(g).wait_recv()

        rows = cot[g]
        n_mb, n_rows, depth = rows.shape
        rows = rows.reshape(n_mb * n_rows, depth)

        @pl.loop(0, feats // f_tile)
        def _(t):
            cols = pl.ds(pl.multiple_of(t * f_tile, f_tile), f_tile)
            res = lax.dot_general(
                cot[g].reshape(n_mb * n_rows, depth),
                w[0, cols, :],
                (((1,), (1,)), ((), ())),
                preferred_element_type=jnp.float32,
            ).reshape(n_mb, per_block, n_rows // per_block, f_tile)
            for s in range(per_block):
                part[g * per_block + s, :, :, cols] = res[:, s]

    def fin_copy(to):
        return pltpu.make_async_remote_copy(
            src_ref=sendbuf.at[to * n_out + k],
            dst_ref=landing.at[i],
            send_sem=fin_s.at[to],
            recv_sem=fin_r.at[i],
            device_id={"tok": to},
            device_id_type=MESH,
        )

    low = 2 * j < n_inc

    def group_first(q):
        r = jnp.maximum(q - 1, 0)
        tail = q > pairs * (n_inc - 1)
        dp = jnp.where(tail, q - pairs * (n_inc - 1), r // max(n_inc - 1, 1))
        dj = jnp.where(tail | (q == 0), 0, 1 + r % max(n_inc - 1, 1))
        return jnp.where(q == 0, 0, dp), dj

    def group_second(q):
        return q % pairs, q // pairs

    def group(q, down):
        first, second = group_first(q), group_second(q)
        use = jnp.logical_not(low) if down else low
        return jnp.where(use, first[0], second[0]), jnp.where(use, first[1], second[1])

    def item_at(q, n, down):
        dp, dj = group(q, down)
        s, dc = n // 2, n % 2
        if not down:
            s = per_block - 1 - s
        jj = inc_at(dj)
        return (tok_at(dp, dc) * n_inc + jj) * per_block + s, jj * per_block + s

    def emit(q):
        for down in range(2):

            @pl.when(k == (n_out - 1 if down else 0))
            def _():
                @pl.loop(0, 2 * per_block)
                def _(n):
                    item, target = item_at(q, n, down)

                    @pl.when(target != k)
                    def _():
                        sendbuf[item] = part[item].astype(jnp.bfloat16)
                        line_copy(item, down).start()

    def finish(dp, dj):
        jj = inc_at(dj)

        @pl.when(jj == k // per_block)
        def _():
            @pl.loop(0, 2)
            def _(dc):
                to = tok_at(dp, dc)
                item = to * n_out + k

                @pl.when(k > 0)
                def _():
                    line_wait(item, 0)
                    part[item] = part[item] + recv[0, item].astype(jnp.float32)

                @pl.when(k < n_out - 1)
                def _():
                    line_wait(item, 1)
                    part[item] = part[item] + recv[1, item].astype(jnp.float32)

                @pl.when(to == i)
                def _():
                    landing[i] = part[item].astype(jnp.bfloat16)

                @pl.when(to != i)
                def _():
                    sendbuf[item] = part[item].astype(jnp.bfloat16)
                    fin_copy(to).start()

    def relay(q):
        @pl.when(jnp.logical_not(at_edge))
        def _():
            @pl.loop(0, 2 * per_block)
            def _(n):
                for down in range(2):
                    item, target = item_at(q, n, down)

                    @pl.when(target < k if down else target > k)
                    def _():
                        line_wait(item, down)
                        sendbuf[item] = (
                            part[item] + recv[down, item].astype(jnp.float32)
                        ).astype(jnp.bfloat16)
                        line_copy(item, down).start()

        dp, dj = group_first(q)

        @pl.when(dj == 0)
        def _():
            finish(dp, dj)

        dp, dj = group_second(q)

        @pl.when(dj > 0)
        def _():
            finish(dp, dj)

    def weight_term(dp, dc):
        to = tok_at(dp, dc)
        if dp or dc:
            pltpu.make_async_remote_copy(
                src_ref=acts.at[to],
                dst_ref=acts.at[to],
                send_sem=act_s.at[dp * 2 + dc],
                recv_sem=act_r.at[to],
                device_id={"tok": tok_at(0, 1)},
                device_id_type=MESH,
            ).wait_recv()
        else:
            act_copy.wait()

    def weight_dot(to):
        @pl.loop(0, feats // f_tile)
        def _(t):
            cols = pl.ds(pl.multiple_of(t * f_tile, f_tile), f_tile)
            n_mb = acts.shape[1]
            lhs = acts[to, :, :, cols].reshape(-1, f_tile)
            rhs = jnp.concatenate(
                [cot[to * n_inc + jj, m] for m in range(n_mb) for jj in range(n_inc)], axis=0
            )
            dw[cols, :] += lax.dot_general(
                lhs, rhs, (((0,), (0,)), ((), ())), preferred_element_type=jnp.float32
            )

    def run(fn, low, high):
        @pl.loop(low, high)
        def _(b):
            fn(b)

    first, groups = min(2 * n_inc + 2, blocks), pairs * n_inc
    run(compute, 0, 2)
    emit(0)
    for dp in range(1, pairs):
        g = tok_at(dp, 0) * n_inc + j
        to_core(g).wait_recv()
        for dj in range(1, n_inc):
            to_inc(dp, dj).start()
        to_core(g).start()
    for dj in range(1, n_inc):
        g = i * n_inc + inc_at(dj)
        to_core(g).wait_recv()
        to_core(g).start()
    run(compute, 2, first)
    emit(1)
    for dp in range(1, pairs):
        for dj in range(1, n_inc):
            g = tok_at(dp, 0) * n_inc + inc_at(dj)
            to_core(g).wait_recv()
            to_core(g).start()
    run(compute, first, blocks)
    run(emit, 2, groups)
    run(relay, 0, 1)
    for dc in range(2):
        weight_term(0, dc)
        weight_dot(tok_at(0, dc))
    run(relay, 1, groups - 1)
    for dp in range(1, pairs):
        for dc in range(2):
            weight_term(dp, dc)
    run(lambda d: weight_dot(tok_at(d // 2, d % 2)), 2, n_tok)
    dw_copy = pltpu.make_async_copy(dw, dw_out.at[0], misc_s.at[2])
    dw_copy.start()
    run(relay, groups - 1, groups)

    def out_copy(frm):
        return pltpu.make_async_copy(
            landing.at[frm],
            dx_out.at[:, :, pl.ds(pl.multiple_of(frm * feats, feats), feats)],
            out_s.at[frm],
        )

    out_copy(i).start()
    for d in range(1, n_tok):
        frm = lax.rem(i + d, n_tok)
        pltpu.make_async_remote_copy(
            src_ref=landing.at[frm],
            dst_ref=landing.at[frm],
            send_sem=fin_s.at[frm],
            recv_sem=fin_r.at[frm],
            device_id={"tok": frm},
            device_id_type=MESH,
        ).wait_recv()
        out_copy(frm).start()

    for dp in range(pairs):
        for dj in range(n_inc):
            to_core(tok_at(dp, 0) * n_inc + inc_at(dj)).wait_send()
            if dj:
                to_inc(dp, dj).wait_send()
        if dp:
            to_tok(dp).wait_send()
        for dc in range(2):
            if dp or dc:
                act_send(dp, dc).wait_send()

    @pl.loop(0, n_tok * n_out)
    def _(item):
        @pl.when(item % n_out != k)
        def _():
            down = jnp.where(item % n_out < k, 1, 0)
            line_copy(item, down).wait_send()

    for d in range(1, n_tok):
        fin_copy(lax.rem(i + d, n_tok)).wait_send()
    for d in range(n_tok):
        out_copy(lax.rem(i + d, n_tok)).wait()
    dw_copy.wait()


def solution(mesh):
    sizes = tuple(mesh.shape[name] for name in ("tok", "inc", "outc"))
    n_tok, n_inc, n_out = sizes

    def local(activations, student_out, teacher_out, weight):
        n_mb, rows, depth = student_out.shape
        feats = weight.shape[1]
        chunk = rows * n_inc // n_out
        items = n_tok * n_out
        bf16, f32 = jnp.bfloat16, jnp.float32
        dma = pltpu.SemaphoreType.DMA
        flops = 4 * n_mb * rows * n_inc * n_tok * depth * feats
        return pl.pallas_call(
            functools.partial(kernel, sizes),
            out_shape=(
                jax.ShapeDtypeStruct((n_mb, chunk, n_tok * feats), bf16),
                jax.ShapeDtypeStruct(weight.shape, f32),
            ),
            in_specs=[
                pl.BlockSpec(memory_space=pl.ANY),
                pl.BlockSpec(memory_space=pltpu.VMEM),
                pl.BlockSpec(memory_space=pltpu.VMEM),
                pl.BlockSpec(memory_space=pl.ANY),
            ],
            out_specs=(pl.BlockSpec(memory_space=pl.ANY), pl.BlockSpec(memory_space=pl.ANY)),
            scratch_shapes=[
                pltpu.VMEM((n_tok * n_inc, n_mb, rows, depth), bf16),
                pltpu.VMEM((n_tok, n_mb, activations.shape[1], feats), bf16),
                pltpu.VMEM((items, n_mb, chunk, feats), f32),
                pltpu.VMEM((2, items, n_mb, chunk, feats), bf16),
                pltpu.VMEM((items, n_mb, chunk, feats), bf16),
                pltpu.VMEM((n_tok, n_mb, chunk, feats), bf16),
                pltpu.VMEM((feats, depth), f32),
                pltpu.VMEM(weight.shape, bf16),
                dma((n_tok * n_inc,)),
                dma((n_tok // 2,)),
                dma((n_tok // 2 * n_inc,)),
                dma((n_tok * n_inc,)),
                dma((n_tok,)),
                dma((n_tok,)),
                dma((items,)),
                dma((2, items)),
                dma((n_tok,)),
                dma((n_tok,)),
                dma((n_tok,)),
                dma((3,)),
            ],
            compiler_params=pltpu.CompilerParams(
                collective_id=0, has_side_effects=True, vmem_limit_bytes=62 * 1024 * 1024
            ),
            cost_estimate=pl.CostEstimate(
                flops=flops, bytes_accessed=16 * 1024 * 1024, transcendentals=0
            ),
        )(activations, student_out, teacher_out, weight)

    placed = (
        P(None, "tok", "inc"),
        P(None, ("tok", "inc"), "outc"),
        P(None, ("tok", "inc"), "outc"),
        P("inc", "tok", "outc"),
    )
    return jax.shard_map(
        local,
        mesh=mesh,
        in_specs=placed,
        out_specs=(P(None, ("tok", "outc"), "inc"), P("inc", "tok", "outc")),
        check_vma=False,
    )
```

```python
import functools

import jax
import jax.numpy as jnp
from jax import lax
from jax.experimental import pallas as pl
from jax.experimental.pallas import tpu as pltpu
from jax.sharding import PartitionSpec as P

MESH = pl.DeviceIdType.MESH


def kernel(
    sizes,
    act,
    student,
    teacher,
    weight,
    dx_out,
    dw_out,
    cot,
    acts,
    part,
    recv,
    sendbuf,
    landing,
    dw,
    w,
    cot_core_s,
    cot_tok_s,
    cot_inc_s,
    cot_r,
    act_s,
    act_r,
    line_s,
    line_r,
    fin_s,
    fin_r,
    out_s,
    misc_s,
):
    n_tok, n_inc, n_out = sizes
    pairs = n_tok // 2
    per_block = n_out // n_inc
    blocks = n_tok * n_inc
    feats = dw.shape[0]
    i, j, k = lax.axis_index("tok"), lax.axis_index("inc"), lax.axis_index("outc")
    p, c = i // 2, i % 2
    f_tile = min(256, feats)

    def tok_at(dp, dc):
        return lax.rem(p + dp, pairs) * 2 + lax.rem(c + dc, 2)

    def inc_at(dj):
        return lax.rem(j + dj, n_inc)

    barrier = pltpu.get_barrier_semaphore()
    for d in range(1, n_tok):
        pl.semaphore_signal(
            barrier, inc=1, device_id={"tok": lax.rem(i + d, n_tok)}, device_id_type=MESH
        )
    for d in range(1, n_inc):
        pl.semaphore_signal(barrier, inc=1, device_id={"inc": inc_at(d)}, device_id_type=MESH)

    @pl.when(k > 0)
    def _():
        pl.semaphore_signal(barrier, inc=1, device_id={"outc": k - 1}, device_id_type=MESH)

    @pl.when(k < n_out - 1)
    def _():
        pl.semaphore_signal(barrier, inc=1, device_id={"outc": k + 1}, device_id_type=MESH)

    own = i * n_inc + j
    w_copy = pltpu.make_async_copy(weight, w, misc_s.at[0])
    w_copy.start()
    act_copy = pltpu.make_async_copy(
        act.at[:, :, pl.ds(pl.multiple_of(i * feats, feats), feats)], acts.at[i], misc_s.at[1]
    )
    act_copy.start()
    cot[own] = (student[...].astype(jnp.float32) - teacher[...].astype(jnp.float32)).astype(
        jnp.bfloat16
    )

    @pl.loop(0, feats // f_tile)
    def _(t):
        rows = pl.ds(pl.multiple_of(t * f_tile, f_tile), f_tile)
        dw[rows, :] = jnp.zeros((f_tile, dw.shape[1]), jnp.float32)

    edges = jnp.where(k > 0, 1, 0) + jnp.where(k < n_out - 1, 1, 0)
    pl.semaphore_wait(barrier, n_tok - 1 + n_inc - 1 + edges)

    def cot_copy(g, sem, device):
        return pltpu.make_async_remote_copy(
            src_ref=cot.at[g],
            dst_ref=cot.at[g],
            send_sem=sem,
            recv_sem=cot_r.at[g],
            device_id=device,
            device_id_type=MESH,
        )

    core = {"tok": tok_at(0, 1)}

    def to_core(g):
        return cot_copy(g, cot_core_s.at[g], core)

    def to_tok(dp):
        return cot_copy(own, cot_tok_s.at[dp], {"tok": tok_at(dp, 0)})

    def to_inc(dp, dj):
        g = tok_at(dp, 0) * n_inc + j
        return cot_copy(g, cot_inc_s.at[dp * n_inc + dj], {"inc": inc_at(dj)})

    def act_send(dp, dc):
        to = tok_at(dp, dc)
        return pltpu.make_async_remote_copy(
            src_ref=act.at[:, :, pl.ds(pl.multiple_of(to * feats, feats), feats)],
            dst_ref=acts.at[i],
            send_sem=act_s.at[dp * 2 + dc],
            recv_sem=act_r.at[i],
            device_id={"tok": to},
            device_id_type=MESH,
        )

    to_core(own).start()
    for dp in range(1, pairs):
        to_tok(dp).start()
    for dj in range(1, n_inc):
        to_inc(0, dj).start()
    for dp in range(pairs):
        for dc in range(2):
            if dp or dc:
                act_send(dp, dc).start()
    w_copy.wait()

    def block_of(b):
        dc, rest = b % 2, b // 2
        dj, dp = rest % n_inc, rest // n_inc
        to, jj = tok_at(dp, dc), inc_at(dj)
        return to, jj, to * n_inc + jj, dc

    def line_copy(item, down):
        return pltpu.make_async_remote_copy(
            src_ref=sendbuf.at[item],
            dst_ref=recv.at[down, item],
            send_sem=line_s.at[item],
            recv_sem=line_r.at[down, item],
            device_id={"outc": k + 1 - 2 * down},
            device_id_type=MESH,
        )

    def line_wait(item, down):
        pltpu.make_async_remote_copy(
            src_ref=sendbuf.at[item],
            dst_ref=recv.at[down, item],
            send_sem=line_s.at[item],
            recv_sem=line_r.at[down, item],
            device_id={"outc": lax.rem(k + 1, n_out)},
            device_id_type=MESH,
        ).wait_recv()

    at_edge = (k == 0) | (k == n_out - 1)

    def compute(b):
        to, jj, g, dc = block_of(b)

        @pl.when(dc == 1)
        def _():
            to_core(g).wait_recv()

        rows = cot[g]
        n_mb, n_rows, depth = rows.shape
        rows = rows.reshape(n_mb * n_rows, depth)

        @pl.loop(0, feats // f_tile)
        def _(t):
            cols = pl.ds(pl.multiple_of(t * f_tile, f_tile), f_tile)
            res = lax.dot_general(
                cot[g].reshape(n_mb * n_rows, depth),
                w[0, cols, :],
                (((1,), (1,)), ((), ())),
                preferred_element_type=jnp.float32,
            ).reshape(n_mb, per_block, n_rows // per_block, f_tile)
            for s in range(per_block):
                part[g * per_block + s, :, :, cols] = res[:, s]

    def fin_copy(to):
        return pltpu.make_async_remote_copy(
            src_ref=sendbuf.at[to * n_out + k],
            dst_ref=landing.at[i],
            send_sem=fin_s.at[to],
            recv_sem=fin_r.at[i],
            device_id={"tok": to},
            device_id_type=MESH,
        )

    low = 2 * j < n_inc

    def group_first(q):
        r = jnp.maximum(q - 1, 0)
        tail = q > pairs * (n_inc - 1)
        dp = jnp.where(tail, q - pairs * (n_inc - 1), r // max(n_inc - 1, 1))
        dj = jnp.where(tail | (q == 0), 0, 1 + r % max(n_inc - 1, 1))
        return jnp.where(q == 0, 0, dp), dj

    def group_second(q):
        return q % pairs, q // pairs

    def group(q, down):
        first, second = group_first(q), group_second(q)
        use = jnp.logical_not(low) if down else low
        return jnp.where(use, first[0], second[0]), jnp.where(use, first[1], second[1])

    def item_at(q, n, down):
        dp, dj = group(q, down)
        s, dc = n // 2, n % 2
        if not down:
            s = per_block - 1 - s
        jj = inc_at(dj)
        return (tok_at(dp, dc) * n_inc + jj) * per_block + s, jj * per_block + s

    def emit(q):
        for down in range(2):

            @pl.when(k == (n_out - 1 if down else 0))
            def _():
                @pl.loop(0, 2 * per_block)
                def _(n):
                    item, target = item_at(q, n, down)

                    @pl.when(target != k)
                    def _():
                        sendbuf[item] = part[item].astype(jnp.bfloat16)
                        line_copy(item, down).start()

    def finish(dp, dj):
        jj = inc_at(dj)

        @pl.when(jj == k // per_block)
        def _():
            @pl.loop(0, 2)
            def _(dc):
                to = tok_at(dp, dc)
                item = to * n_out + k

                @pl.when(k > 0)
                def _():
                    line_wait(item, 0)
                    part[item] = part[item] + recv[0, item].astype(jnp.float32)

                @pl.when(k < n_out - 1)
                def _():
                    line_wait(item, 1)
                    part[item] = part[item] + recv[1, item].astype(jnp.float32)

                @pl.when(to == i)
                def _():
                    landing[i] = part[item].astype(jnp.bfloat16)

                @pl.when(to != i)
                def _():
                    sendbuf[item] = part[item].astype(jnp.bfloat16)
                    fin_copy(to).start()

    def relay(q):
        @pl.when(jnp.logical_not(at_edge))
        def _():
            @pl.loop(0, 2 * per_block)
            def _(n):
                for down in range(2):
                    item, target = item_at(q, n, down)

                    @pl.when(target < k if down else target > k)
                    def _():
                        line_wait(item, down)
                        sendbuf[item] = (
                            part[item] + recv[down, item].astype(jnp.float32)
                        ).astype(jnp.bfloat16)
                        line_copy(item, down).start()

    def finish_group(q):
        dp, dj = group_first(q)

        @pl.when(dj == 0)
        def _():
            finish(dp, dj)

        dp, dj = group_second(q)

        @pl.when(dj > 0)
        def _():
            finish(dp, dj)

    def weight_term(dp, dc):
        to = tok_at(dp, dc)
        if dp or dc:
            pltpu.make_async_remote_copy(
                src_ref=acts.at[to],
                dst_ref=acts.at[to],
                send_sem=act_s.at[dp * 2 + dc],
                recv_sem=act_r.at[to],
                device_id={"tok": tok_at(0, 1)},
                device_id_type=MESH,
            ).wait_recv()
        else:
            act_copy.wait()

    def weight_dot(to):
        @pl.loop(0, feats // f_tile)
        def _(t):
            cols = pl.ds(pl.multiple_of(t * f_tile, f_tile), f_tile)
            n_mb = acts.shape[1]
            lhs = acts[to, :, :, cols].reshape(-1, f_tile)
            rhs = jnp.concatenate(
                [cot[to * n_inc + jj, m] for m in range(n_mb) for jj in range(n_inc)], axis=0
            )
            dw[cols, :] += lax.dot_general(
                lhs, rhs, (((0,), (0,)), ((), ())), preferred_element_type=jnp.float32
            )

    def run(fn, low, high):
        @pl.loop(low, high)
        def _(b):
            fn(b)

    first, groups = min(2 * n_inc + 2, blocks), pairs * n_inc
    run(compute, 0, 2)
    emit(0)
    for dp in range(1, pairs):
        g = tok_at(dp, 0) * n_inc + j
        to_core(g).wait_recv()
        for dj in range(1, n_inc):
            to_inc(dp, dj).start()
        to_core(g).start()
    for dj in range(1, n_inc):
        g = i * n_inc + inc_at(dj)
        to_core(g).wait_recv()
        to_core(g).start()
    run(compute, 2, first)
    emit(1)
    relay(0)
    for dp in range(1, pairs):
        for dj in range(1, n_inc):
            g = tok_at(dp, 0) * n_inc + inc_at(dj)
            to_core(g).wait_recv()
            to_core(g).start()
    run(compute, first, blocks)
    run(emit, 2, groups)
    run(relay, 1, 2)
    finish_group(0)
    run(relay, 2, groups)
    for dc in range(2):
        weight_term(0, dc)
        weight_dot(tok_at(0, dc))
    run(finish_group, 1, groups - 1)
    for dp in range(1, pairs):
        for dc in range(2):
            weight_term(dp, dc)
    run(lambda d: weight_dot(tok_at(d // 2, d % 2)), 2, n_tok)
    dw_copy = pltpu.make_async_copy(dw, dw_out.at[0], misc_s.at[2])
    dw_copy.start()
    run(finish_group, groups - 1, groups)

    def out_copy(frm):
        return pltpu.make_async_copy(
            landing.at[frm],
            dx_out.at[:, :, pl.ds(pl.multiple_of(frm * feats, feats), feats)],
            out_s.at[frm],
        )

    out_copy(i).start()
    for d in range(1, n_tok):
        frm = lax.rem(i + d, n_tok)
        pltpu.make_async_remote_copy(
            src_ref=landing.at[frm],
            dst_ref=landing.at[frm],
            send_sem=fin_s.at[frm],
            recv_sem=fin_r.at[frm],
            device_id={"tok": frm},
            device_id_type=MESH,
        ).wait_recv()
        out_copy(frm).start()

    for dp in range(pairs):
        for dj in range(n_inc):
            to_core(tok_at(dp, 0) * n_inc + inc_at(dj)).wait_send()
            if dj:
                to_inc(dp, dj).wait_send()
        if dp:
            to_tok(dp).wait_send()
        for dc in range(2):
            if dp or dc:
                act_send(dp, dc).wait_send()

    @pl.loop(0, n_tok * n_out)
    def _(item):
        @pl.when(item % n_out != k)
        def _():
            down = jnp.where(item % n_out < k, 1, 0)
            line_copy(item, down).wait_send()

    for d in range(1, n_tok):
        fin_copy(lax.rem(i + d, n_tok)).wait_send()
    for d in range(n_tok):
        out_copy(lax.rem(i + d, n_tok)).wait()
    dw_copy.wait()


def solution(mesh):
    sizes = tuple(mesh.shape[name] for name in ("tok", "inc", "outc"))
    n_tok, n_inc, n_out = sizes

    def local(activations, student_out, teacher_out, weight):
        n_mb, rows, depth = student_out.shape
        feats = weight.shape[1]
        chunk = rows * n_inc // n_out
        items = n_tok * n_out
        bf16, f32 = jnp.bfloat16, jnp.float32
        dma = pltpu.SemaphoreType.DMA
        flops = 4 * n_mb * rows * n_inc * n_tok * depth * feats
        return pl.pallas_call(
            functools.partial(kernel, sizes),
            out_shape=(
                jax.ShapeDtypeStruct((n_mb, chunk, n_tok * feats), bf16),
                jax.ShapeDtypeStruct(weight.shape, f32),
            ),
            in_specs=[
                pl.BlockSpec(memory_space=pl.ANY),
                pl.BlockSpec(memory_space=pltpu.VMEM),
                pl.BlockSpec(memory_space=pltpu.VMEM),
                pl.BlockSpec(memory_space=pl.ANY),
            ],
            out_specs=(pl.BlockSpec(memory_space=pl.ANY), pl.BlockSpec(memory_space=pl.ANY)),
            scratch_shapes=[
                pltpu.VMEM((n_tok * n_inc, n_mb, rows, depth), bf16),
                pltpu.VMEM((n_tok, n_mb, activations.shape[1], feats), bf16),
                pltpu.VMEM((items, n_mb, chunk, feats), f32),
                pltpu.VMEM((2, items, n_mb, chunk, feats), bf16),
                pltpu.VMEM((items, n_mb, chunk, feats), bf16),
                pltpu.VMEM((n_tok, n_mb, chunk, feats), bf16),
                pltpu.VMEM((feats, depth), f32),
                pltpu.VMEM(weight.shape, bf16),
                dma((n_tok * n_inc,)),
                dma((n_tok // 2,)),
                dma((n_tok // 2 * n_inc,)),
                dma((n_tok * n_inc,)),
                dma((n_tok,)),
                dma((n_tok,)),
                dma((items,)),
                dma((2, items)),
                dma((n_tok,)),
                dma((n_tok,)),
                dma((n_tok,)),
                dma((3,)),
            ],
            compiler_params=pltpu.CompilerParams(
                collective_id=0, has_side_effects=True, vmem_limit_bytes=62 * 1024 * 1024
            ),
            cost_estimate=pl.CostEstimate(
                flops=flops, bytes_accessed=16 * 1024 * 1024, transcendentals=0
            ),
        )(activations, student_out, teacher_out, weight)

    placed = (
        P(None, "tok", "inc"),
        P(None, ("tok", "inc"), "outc"),
        P(None, ("tok", "inc"), "outc"),
        P("inc", "tok", "outc"),
    )
    return jax.shard_map(
        local,
        mesh=mesh,
        in_specs=placed,
        out_specs=(P(None, ("tok", "outc"), "inc"), P("inc", "tok", "outc")),
        check_vma=False,
    )
```
